32 devices in a mesh: fsdp: 8 (over z, y), tensor: 4 (over x, core).
Axes of the slice: x: 2, y: 2, z: 4, core: 2. Of those that a mesh axis runs over, the one named last changes fastest.
Arguments:
- tokens: bfloat16 [256, 4096], P(('fsdp', 'tensor')), may hold values from -6 to 6
- weight: bfloat16 [4096, 14336], P('fsdp', 'tensor'), may hold values from -0.25 to 0.25
- tile_pick: int32 [32, 16], replicated, may hold values from -1 to 6
- cotangent: bfloat16 [256, 14336], P('fsdp', 'tensor'), may hold values from -6 to 6
Outputs:
- activated: bfloat16 [256, 14336], P('fsdp', 'tensor')
- token_grad: bfloat16 [256, 4096], P(('fsdp', 'tensor'))
- weight_grad: float32 [4096, 14336], P('fsdp', 'tensor')
The draws below stay inside these ranges and needn't reach their ends.
Inputs may be any that keep to these rules, and one draw needn't show every extreme that they name: tile_pick[r, g] is the kept tile among the 7 tiles of column group g in tile row r, or -1 when none of them is kept.
All inputs are finite; a program needn't handle non-finite values.
Results may differ from the reference program's by a relative error of at most 0.013.
Values may be sent and summed in bfloat16 or wider, within the bound.
No kernel may reach another device: no remote copies, remote signals or barrier semaphores. Data moves between devices by JAX's collectives and lax.ppermute only.
A program may use at most 64 MiB of HBM per device.

```python
import math
import jax
import jax.numpy as jnp
from jax import lax

D = 4096
F = 14336
TILE = 128
GROUP = 7
TOKENS = 256
TILE_ROWS = 32
GROUPS = 16
N_TENSOR = 4


def plant(array, rng, low, largest):
    extent = array.shape
    place = [jax.random.randint(jax.random.fold_in(rng, axis), (), 0, extent[axis]) for axis in range(len(extent))]
    array = array.at[tuple(place)].set(low)
    longest = extent.index(max(extent))
    place[longest] = (place[longest] + 1) % extent[longest]
    return array.at[tuple(place)].set(largest)


def raised(result, stream_key, source, target, shards_of, factor):
    owner, partner = [(jnp.arange(result.shape[dim]) // (result.shape[dim] // shards_of)).reshape([-1 if axis == dim else 1 for axis in range(result.ndim)]) for dim in (source, target)]
    chosen = jax.random.permutation(stream_key, shards_of)[partner]
    strong = (owner == chosen) | (owner == (partner + shards_of // 2) % shards_of)
    return jnp.where(strong, factor * result, result)


def level_of(stream_key, extent, shards, smallest, top_value):
    loudness = 1.0
    for position, shards_of in shards:
        draws = jax.random.uniform(jax.random.fold_in(jax.random.fold_in(stream_key, 6), position), (shards_of,), jnp.float32, smallest / len(shards), top_value / len(shards))
        loudness = loudness * jnp.repeat(jnp.exp(draws), extent[position] // shards_of).reshape((-1,) + (1,) * (len(extent) - 1 - position))
    return loudness


def centred(key, extent, width, reach, shards=(), held_as=jnp.bfloat16):
    level = level_of(key, extent, shards, -0.22, 0.18) if shards else 1.0
    values = jax.random.normal(key, extent, jnp.float32) * width * level
    return jnp.minimum(jnp.maximum(values, -reach), reach).astype(held_as)


def gaussian_with(rng, shape, width, bound, cuts, heavy, held_as=jnp.bfloat16):
    result = width * jax.random.normal(rng, shape, jnp.float32)
    if cuts:
        result = result * level_of(rng, shape, cuts, -0.22, 0.18)
    return jnp.clip(raised(result, jax.random.fold_in(rng, 3), *heavy), -bound, bound).astype(held_as)


def setup_inputs(seed: int = 0) -> dict:
    seeds = jax.random.split(jax.random.key(seed), 5)
    tokens = gaussian_with(seeds[0], (TOKENS, D), 1.0, 6.0, ((0, 32),), (0, 1, 32, 2.75))
    weight = centred(seeds[1], (D, F), (D // (GROUP + 1)) ** -0.5, 0.25, ((0, 8), (1, 4)))
    tile_pick = plant(jax.random.randint(seeds[2], (TILE_ROWS, GROUPS), -1, GROUP), jax.random.fold_in(seeds[2], 1), -1, GROUP - 1).astype(jnp.int32)
    cotangent = centred(seeds[3], (TOKENS, F), 1.0, 6.0, ((0, 8), (1, 4)))
    return {"tokens": tokens, "weight": weight, "tile_pick": tile_pick, "cotangent": cotangent}


precise_mode = lax.Precision.HIGHEST


def reference(tokens, weight, tile_pick, cotangent):
    tile_rows = D // TILE
    groups = F // (TILE * GROUP)
    slots = groups // N_TENSOR
    block_len = math.gcd(TOKENS, 512)
    blocks = TOKENS // block_len
    onehot = (tile_pick[:, :, None] == jnp.arange(GROUP, dtype=jnp.int32)[None, None, :]).astype(jnp.float32)
    weight_five = weight.astype(jnp.float32).reshape(tile_rows, TILE, groups, GROUP, TILE)
    packed = jnp.einsum('rkgjn,rgj->rkgn', weight_five, onehot, precision=precise_mode).astype(jnp.bfloat16)
    packed_f = packed.astype(jnp.float32)
    packed_split = packed_f.reshape(tile_rows, TILE, N_TENSOR, slots, TILE)

    def one_block(running, inputs):
        tok_block, cot_block = inputs
        tok_three = tok_block.astype(jnp.float32).reshape(block_len, tile_rows, TILE)
        partial_value = jnp.einsum('trk,rkgn->trgn', tok_three, packed_f, precision=precise_mode)
        pre_act = jnp.einsum('trgn,rgj->tgjn', partial_value, onehot, precision=precise_mode).reshape(block_len, F)
        sigmoid_pre = jax.nn.sigmoid(pre_act)
        activated = (pre_act * sigmoid_pre).astype(jnp.bfloat16)
        dpre = (cot_block.astype(jnp.float32) * sigmoid_pre * (1.0 + pre_act * (1.0 - sigmoid_pre))).astype(jnp.bfloat16)
        dpre_four = dpre.astype(jnp.float32).reshape(block_len, groups, GROUP, TILE)
        dpacked = jnp.einsum('tgjn,rgj->trgn', dpre_four, onehot, precision=precise_mode).astype(jnp.bfloat16)
        dpacked_f = dpacked.astype(jnp.float32)
        per_panel = jnp.einsum('trpsn,rkpsn->tprk', dpacked_f.reshape(block_len, tile_rows, N_TENSOR, slots, TILE), packed_split, precision=precise_mode)
        per_panel = lax.optimization_barrier(per_panel.astype(jnp.bfloat16)).astype(jnp.float32)
        token_grad = jnp.sum(per_panel, axis=1).reshape(block_len, D).astype(jnp.bfloat16)
        running = running + jnp.einsum('trk,trgn->rkgn', tok_three, dpacked_f, precision=precise_mode)
        return running, (activated, token_grad)

    start_sum = jnp.zeros((tile_rows, TILE, groups, TILE), jnp.float32)
    tok_blocks = tokens.reshape(blocks, block_len, D)
    cot_blocks = cotangent.reshape(blocks, block_len, F)
    tile_sums, (act_blocks, grad_blocks) = lax.scan(one_block, start_sum, (tok_blocks, cot_blocks))
    weight_grad = (tile_sums[:, :, :, None, :] * onehot[:, None, :, :, None]).reshape(D, F)
    return act_blocks.reshape(TOKENS, F), grad_blocks.reshape(TOKENS, D), weight_grad
```

```python
import functools
import math

import jax
import jax.numpy as jnp
from jax import lax
from jax.experimental import pallas as pl
from jax.experimental.pallas import tpu as pltpu
from jax.sharding import PartitionSpec as P

TILE = 128
GROUP = 7
CHUNKS = 1


precise_mode = lax.Precision.HIGHEST
f32, bf16 = jnp.float32, jnp.bfloat16
VMEM = pl.BlockSpec(memory_space=pltpu.VMEM)
SMEM = pl.BlockSpec(memory_space=pltpu.SMEM)
ANY = pl.BlockSpec(memory_space=pl.ANY)


def sds(shape, dtype):
    return jax.ShapeDtypeStruct(shape, dtype)


def call(body, name, ins, outs, scratch=(), flops=0, moved=0):
    return pl.pallas_call(
        body,
        name=name,
        out_shape=outs,
        in_specs=ins,
        out_specs=jax.tree.map(lambda _: VMEM, outs),
        scratch_shapes=scratch,
        cost_estimate=pl.CostEstimate(flops=flops, bytes_accessed=moved, transcendentals=0),
    )


def shift(x, axis, k):
    n = lax.axis_size(axis)
    return lax.ppermute(x, axis, [(i, i ^ k) for i in range(n)])


def cols(tile):
    return pl.ds(tile * TILE, TILE)


def resident_plan(tokens, weight, tile_pick, cotangent):
    nf, nt = lax.axis_size("fsdp"), lax.axis_size("tensor")
    half = nf // 2
    near = range(half)
    rows, panel = weight.shape
    feat = tokens.shape[1]
    group = cotangent.shape[0]
    mine = tokens.shape[0]
    tr = rows // TILE
    slots = panel // (TILE * GROUP)
    chunks = math.gcd(CHUNKS, slots)
    sc = slots // chunks
    nt_tiles = sc * GROUP
    half_tokens = half * group

    def where_am_i():
        return lax.axis_index("fsdp"), lax.axis_index("tensor")

    def pick_of(pick, row, slot):
        return jnp.maximum(pick[row, slot], 0)

    def pack_body(pick, w, *rest):
        outs, sem = rest[:chunks], rest[chunks]
        f, t = where_am_i()
        copies = []
        for i in range(tr):
            for s in range(slots):
                j = pick_of(pick, f * tr + i, t * slots + s)
                at = pl.ds(pl.multiple_of((s * GROUP + j) * TILE, TILE), TILE)
                cp = pltpu.make_async_copy(
                    w.at[pl.ds(i * TILE, TILE), at],
                    outs[s // sc].at[pl.ds(i * TILE, TILE), cols(s % sc)],
                    sem.at[i * slots + s],
                )
                cp.start()
                copies.append(cp)
        for cp in copies:
            cp.wait()
        for i in range(tr):
            for s in range(slots):

                @pl.when(pick[f * tr + i, t * slots + s] < 0)
                def _():
                    outs[s // sc][pl.ds(i * TILE, TILE), cols(s % sc)] = jnp.zeros((TILE, TILE), bf16)

    own_w = call(
        pack_body, "pack", [SMEM, ANY], [sds((rows, sc * TILE), bf16)] * chunks,
        [pltpu.SemaphoreType.DMA((tr * slots,))], moved=4 * rows * slots * TILE,
    )(tile_pick, weight)
    far_w = [shift(w, "fsdp", half) for w in own_w]

    gathered = lax.all_gather(tokens, "tensor", axis=0, tiled=True)

    def cut_body(x, *outs):
        f, _ = where_am_i()
        for k in near:
            for h in range(2):
                d = jnp.bitwise_xor(f, k + h * half)
                outs[k][:, pl.ds(h * rows, rows)] = x[:, pl.ds(pl.multiple_of(d * rows, TILE), rows)]

    cut = call(cut_body, "cut", [VMEM], [sds((group, 2 * rows), bf16)] * half, moved=4 * group * feat)(gathered)
    tok = [cut[k] if k == 0 else shift(cut[k], "fsdp", k) for k in near]

    def forward_body(c, pick, *rest):
        toks, (w_own, w_far) = rest[:half], rest[half : half + 2]
        outs = rest[half + 2 : half + 2 + half]
        tokfar = rest[2 * half + 2] if c == 0 else None
        xs, acc = rest[-2:]
        f, t = where_am_i()
        acc[...] = jnp.zeros_like(acc)
        for k in near:
            xs[pl.ds(k * group, group), :] = toks[k][...]
        if tokfar is not None:
            for k in near:
                tokfar[k] = toks[k][:, pl.ds(rows, rows)]
        for h, w in enumerate((w_own, w_far)):
            owner = jnp.bitwise_xor(f, h * half)
            for i in range(tr):
                y = jnp.dot(
                    xs[:, pl.ds(h * rows + i * TILE, TILE)],
                    w[pl.ds(i * TILE, TILE), :],
                    preferred_element_type=f32,
                )
                for s in range(sc):
                    j = pick_of(pick, owner * tr + i, t * slots + c * sc + s)
                    acc[s * GROUP + j] += y[:, s * TILE : (s + 1) * TILE]
        for k in near:
            outs[k][...] = acc[:, pl.ds(k * group, group), :].astype(outs[k].dtype)

    dense = (nt_tiles, group, TILE)
    pre_parts, tok_far = [], None
    for c in range(chunks):
        outs = [sds(dense, f32)] + [sds(dense, bf16)] * (half - 1)
        if c == 0:
            outs.append(sds((half, group, rows), bf16))
        got = call(
            functools.partial(forward_body, c), f"forward{c}", [SMEM] + [VMEM] * (half + 2), outs,
            [pltpu.VMEM((half_tokens, 2 * rows), bf16), pltpu.VMEM((nt_tiles, half_tokens, TILE), f32)],
            flops=4 * half_tokens * rows * sc * TILE, moved=8 * half_tokens * nt_tiles * TILE,
        )(tile_pick, *tok, own_w[c], far_w[c])
        if c == 0:
            tok_far = got[half]
        pre_parts.append([got[0]] + [shift(got[k], "fsdp", k) for k in near[1:]])

    def act_body(c, pick, *rest):
        parts, cot = rest[:half], rest[half]
        prev = rest[half + 1 : half + 1 + (c if c == chunks - 1 else 0)]
        act, d = rest[half + 1 + len(prev)], rest[half + 2 + len(prev)]
        fars = rest[half + 3 + len(prev) :]
        f, t = where_am_i()
        base = 0
        if prev:
            for q, p in enumerate(prev):
                act[:, pl.ds(q * nt_tiles * TILE, nt_tiles * TILE)] = p[...]
            base = c * nt_tiles
        for g in range(nt_tiles):
            pre = parts[0][g]
            for k in near[1:]:
                pre = pre + parts[k][g].astype(f32)
            s = jax.nn.sigmoid(pre)
            act[:, cols(base + g)] = (pre * s).astype(bf16)
            cg = cot[:, cols(c * nt_tiles + g)].astype(f32)
            d[g] = (cg * s * (1.0 + pre * (1.0 - s))).astype(bf16)
        for q, far in enumerate(fars):
            owner = jnp.bitwise_xor(f, half + q)
            for i in range(tr):
                for s in range(sc):
                    j = pick_of(pick, owner * tr + i, t * slots + c * sc + s)
                    far[i, :, cols(s)] = d[s * GROUP + j]

    acts, d_near, d_far = [], [], []
    for c in range(chunks):
        last = c == chunks - 1
        width = panel if last else nt_tiles * TILE
        prev = acts if last else []
        outs = [sds((group, width), bf16), sds(dense, bf16)] + [sds((tr, group, sc * TILE), bf16)] * half
        got = call(
            functools.partial(act_body, c), f"act{c}", [SMEM] + [VMEM] * (half + 1 + len(prev)), outs,
            flops=20 * group * nt_tiles * TILE, moved=16 * group * nt_tiles * TILE,
        )(tile_pick, *pre_parts[c], cotangent, *prev)
        acts.append(got[0])
        d_near.append([got[1]] + [shift(got[1], "fsdp", k) for k in near[1:]])
        d_far.append([shift(got[2 + q], "fsdp", half + q) for q in near])
    activated = acts[-1]

    def tgrad_body(pick, *rest):
        ds_ = [rest[c * half : (c + 1) * half] for c in range(chunks)]
        at = chunks * half
        ws = (rest[at : at + chunks], rest[at + chunks : at + 2 * chunks])
        outs = rest[at + 2 * chunks : at + 2 * chunks + nt]
        dg, part, tmp = rest[-3:]
        f, t = where_am_i()
        for h in range(2):
            owner = jnp.bitwise_xor(f, h * half)
            for i in range(tr):
                y = None
                for c in range(chunks):
                    for s in range(sc):
                        j = pick_of(pick, owner * tr + i, t * slots + c * sc + s)
                        for k in near:
                            dg[i % 2, pl.ds(k * group, group), cols(c * sc + s)] = ds_[c][k][s * GROUP + j]
                    z = lax.dot_general(
                        dg[i % 2, :, pl.ds(c * sc * TILE, sc * TILE)],
                        ws[h][c][pl.ds(i * TILE, TILE), :],
                        (((1,), (1,)), ((), ())),
                        preferred_element_type=f32,
                    )
                    y = z if y is None else y + z
                part[:, pl.ds(h * rows + i * TILE, TILE)] = y
        for q in range(nt):
            to = jnp.bitwise_xor(t, q)
            for k in near:
                tmp[pl.ds(k * mine, mine), :] = part[pl.ds(pl.multiple_of(k * group + to * mine, 8), mine), :]
            outs[q][...] = tmp[...].astype(bf16)

    flat_d = [d_near[c][k] for c in range(chunks) for k in near]
    parts = call(
        tgrad_body, "tgrad", [SMEM] + [VMEM] * (len(flat_d) + 2 * chunks),
        [sds((half * mine, 2 * rows), bf16)] * nt,
        [
            pltpu.VMEM((2, half_tokens, slots * TILE), bf16),
            pltpu.VMEM((half_tokens, 2 * rows), f32),
            pltpu.VMEM((half * mine, 2 * rows), f32),
        ],
        flops=4 * half_tokens * rows * slots * TILE, moved=4 * half_tokens * panel,
    )(tile_pick, *flat_d, *own_w, *far_w)
    parts = [p if q == 0 else shift(p, "tensor", q) for q, p in enumerate(parts)]

    def sum_body(*refs):
        ins, outs, tmp = refs[:nt], refs[nt : nt + half], refs[-1]
        total = ins[0][...].astype(f32)
        for r in ins[1:]:
            total = total + r[...].astype(f32)
        tmp[...] = total
        for k in near:
            outs[k][...] = tmp[pl.ds(k * mine, mine), :].astype(bf16)

    sums = call(
        sum_body, "tsum", [VMEM] * nt, [sds((mine, 2 * rows), bf16)] * half,
        [pltpu.VMEM((half * mine, 2 * rows), f32)], moved=4 * nt * half * mine * rows,
    )(*parts)
    sums = [s if k == 0 else shift(s, "fsdp", k) for k, s in enumerate(sums)]

    def place_body(*refs):
        ins, out = refs[:half], refs[half]
        f, _ = where_am_i()
        for k in near:
            for h in range(2):
                d = jnp.bitwise_xor(f, k + h * half)
                out[:, pl.ds(pl.multiple_of(d * rows, TILE), rows)] = ins[k][:, pl.ds(h * rows, rows)]

    token_grad = call(place_body, "place", [VMEM] * half, sds((mine, feat), bf16), moved=4 * mine * feat)(*sums)

    tok_far = shift(tok_far, "fsdp", half)

    def wgrad_body(pick, *rest):
        toks, tokfar = rest[:half], rest[half]
        at = half + 1
        dn = [rest[at + c * half : at + (c + 1) * half] for c in range(chunks)]
        at += chunks * half
        df = [rest[at + c * half : at + (c + 1) * half] for c in range(chunks)]
        out, xs, dg = rest[-3:]
        f, t = where_am_i()
        i = pl.program_id(0)
        lane = pl.ds(pl.multiple_of(i * TILE, TILE), TILE)
        for k in near:
            xs[pl.ds(k * group, group), :] = toks[k][:, lane]
            xs[pl.ds((half + k) * group, group), :] = tokfar[k, :, lane]
            for c in range(chunks):
                dg[pl.ds((half + k) * group, group), pl.ds(c * sc * TILE, sc * TILE)] = df[c][k][i]
        for c in range(chunks):
            for s in range(sc):
                j = pick_of(pick, f * tr + i, t * slots + c * sc + s)
                for k in near:
                    dg[pl.ds(k * group, group), cols(c * sc + s)] = dn[c][k][s * GROUP + j]
        y = lax.dot_general(xs[...], dg[...], (((0,), (0,)), ((), ())), preferred_element_type=f32)
        for s in range(slots):
            j = pick[f * tr + i, t * slots + s]
            block = y[:, s * TILE : (s + 1) * TILE]
            for g in range(GROUP):
                out[:, cols(s * GROUP + g)] = jnp.where(j == g, block, 0.0)

    flat_far = [d_far[c][k] for c in range(chunks) for k in near]
    whole = lambda x: pl.BlockSpec(x.shape, lambda i, n=x.ndim: (0,) * n)
    operands = [*tok, tok_far, *flat_d, *flat_far]
    weight_grad = pl.pallas_call(
        wgrad_body,
        name="wgrad",
        grid=(tr,),
        out_shape=sds((rows, panel), f32),
        in_specs=[SMEM] + [whole(x) for x in operands],
        out_specs=pl.BlockSpec((TILE, panel), lambda i: (i, 0)),
        scratch_shapes=[pltpu.VMEM((nf * group, TILE), bf16), pltpu.VMEM((nf * group, slots * TILE), bf16)],
        cost_estimate=pl.CostEstimate(
            flops=2 * nf * group * rows * slots * TILE, bytes_accessed=4 * rows * panel, transcendentals=0
        ),
    )(tile_pick, *operands)
    return activated, token_grad, weight_grad


def gather_plan(tokens, weight, tile_pick, cotangent):
    local_rows, panel_cols = weight.shape
    tile_rows = tile_pick.shape[0]
    feat_width = tokens.shape[1]
    group_rows = cotangent.shape[0]
    slots = panel_cols // (TILE * GROUP)
    packed_cols = slots * TILE
    fsdp_pos = lax.axis_index("fsdp")
    tensor_pos = lax.axis_index("tensor")
    my_picks = lax.dynamic_slice_in_dim(tile_pick, tensor_pos * slots, slots, 1)
    onehot = (my_picks[:, :, None] == jnp.arange(GROUP, dtype=jnp.int32)[None, None, :]).astype(
        jnp.float32
    )
    onehot_half = onehot.astype(jnp.bfloat16)
    row_tile = (fsdp_pos * local_rows + jnp.arange(local_rows, dtype=jnp.int32)) // TILE
    row_match = (row_tile[:, None] == jnp.arange(tile_rows, dtype=jnp.int32)[None, :]).astype(
        jnp.float32
    )
    row_pick = jnp.einsum("rq,qsj->rsj", row_match, onehot, precision=precise_mode)
    local_packed = jnp.einsum(
        "rsjn,rsj->rsn",
        weight.reshape(local_rows, slots, GROUP, TILE),
        row_pick.astype(jnp.bfloat16),
        preferred_element_type=jnp.float32,
    )
    local_packed = local_packed.astype(jnp.bfloat16).reshape(local_rows, packed_cols)
    panel = lax.all_gather(local_packed, "fsdp", axis=0, tiled=True)
    panel_three = panel.reshape(tile_rows, TILE, packed_cols)
    gathered = lax.all_gather(tokens, "tensor", axis=0, tiled=True)
    length = gathered.shape[0]
    partial_value = jnp.einsum(
        "trk,rkm->trm",
        gathered.reshape(length, tile_rows, TILE),
        panel_three,
        preferred_element_type=jnp.float32,
    )
    spread = jnp.einsum(
        "trsn,rsj->tsjn",
        partial_value.reshape(length, tile_rows, slots, TILE),
        onehot,
        precision=precise_mode,
    )
    pre_act = spread.reshape(length, panel_cols)
    sigmoid_pre = jax.nn.sigmoid(pre_act)
    activated = (pre_act * sigmoid_pre).astype(jnp.bfloat16)
    dpre = (
        cotangent.astype(jnp.float32) * sigmoid_pre * (1.0 + pre_act * (1.0 - sigmoid_pre))
    ).astype(jnp.bfloat16)
    dpacked = jnp.einsum(
        "tsjn,rsj->trsn",
        dpre.reshape(group_rows, slots, GROUP, TILE),
        onehot_half,
        preferred_element_type=jnp.float32,
    )
    dpacked = dpacked.astype(jnp.bfloat16).reshape(group_rows, tile_rows, packed_cols)
    partial_value = jnp.einsum(
        "trm,rkm->trk", dpacked, panel_three, preferred_element_type=jnp.float32
    ).reshape(tokens.shape[0] * lax.axis_size("tensor"), feat_width)
    token_grad = lax.psum_scatter(
        lax.optimization_barrier(partial_value.astype(jnp.bfloat16))
        .astype(jnp.float32)
        .astype(jnp.bfloat16),
        "tensor",
        scatter_dimension=0,
        tiled=True,
    )
    tile_sums = jnp.einsum(
        "trk,trm->rkm",
        gathered.reshape(group_rows, tile_rows, TILE),
        dpacked,
        preferred_element_type=jnp.float32,
    )
    my_tiles = lax.psum_scatter(
        tile_sums.reshape(feat_width, packed_cols), "fsdp", scatter_dimension=0, tiled=True
    )
    weight_grad = (my_tiles.reshape(local_rows, slots, 1, TILE) * row_pick[:, :, :, None]).reshape(
        local_rows, panel_cols
    )
    return (activated, token_grad, weight_grad)


def per_device(tokens, weight, tile_pick, cotangent):
    nf, nt = lax.axis_size("fsdp"), lax.axis_size("tensor")
    rows, panel = weight.shape
    group = cotangent.shape[0]
    whole_tiles = rows % TILE == 0 and tokens.shape[0] % 8 == 0 and group % 16 == 0
    paired = nf >= 4 and nf & (nf - 1) == 0 and nt & (nt - 1) == 0
    resident = 2 * 2 * nf * group * panel
    gathered = (2 + 4) * tokens.shape[1] * (panel // GROUP)
    if whole_tiles and paired and resident < gathered:
        return resident_plan(tokens, weight, tile_pick, cotangent)
    return gather_plan(tokens, weight, tile_pick, cotangent)


def solution(mesh):
    placed = (P(("fsdp", "tensor"), None), P("fsdp", "tensor"), P(), P("fsdp", "tensor"))
    return jax.shard_map(
        per_device,
        mesh=mesh,
        in_specs=placed,
        out_specs=(P("fsdp", "tensor"), P(("fsdp", "tensor"), None), P("fsdp", "tensor")),
        check_vma=False,
    )
```
